32 devices in a mesh: section: 4 (over y, x), ep: 8 (over z, core).
Axes of the slice: x: 2, y: 2, z: 4, core: 2. Of those that a mesh axis runs over, the one named last changes fastest.
Arguments:
- handed: bfloat16 [4, 2, 512, 7168], P('section', None, 'ep'), may hold values from -6 to 6
- routes: int32 [4, 2, 512, 2], P('section', None, 'ep'), may hold values from 0 to 3, all different within a row; in each aligned block of 64 rows (0 to 63, 64 to 127, ..., all dimensions but the last counted through in order) at most 36 rows name the same one
- slot_order: int32 [4, 2, 8, 64], P('section', None, 'ep'), may hold values from 0 to 63, each once within a row
- gate_probs: float32 [4, 2, 512, 2], P('section', None, 'ep'), may hold values from 0.2 to 1
- saved_gate: bfloat16 [4, 2, 8, 8, 36, 512], P('section', None, 'ep'), may hold values from -6 to 6
- saved_up: bfloat16 [4, 2, 8, 8, 36, 512], P('section', None, 'ep'), may hold values from -6 to 6
- w_gate: bfloat16 [4, 8, 3584, 1024], P('section', 'ep'), may hold values from -0.0625 to 0.0625
- w_up: bfloat16 [4, 8, 3584, 1024], P('section', 'ep'), may hold values from -0.0625 to 0.0625
- w_down: bfloat16 [4, 8, 1024, 3584], P('section', 'ep'), may hold values from -0.1875 to 0.1875
Outputs:
- grad_in: bfloat16 [4, 2, 512, 7168], P('section', None, 'ep')
The draws below stay inside these ranges and needn't reach their ends.
Inputs may be any that keep to these rules, and one draw needn't show every extreme that they name: `routes`: each row names 2 different experts; within the 64 rows of one device for one direction no expert is named by more than 36 rows, and in some such blocks one expert is named by exactly 36. `slot_order`: within one device and direction each of 0 to 63 stands once.
All inputs are finite; a program needn't handle non-finite values.
Results may differ from the reference program's by a relative error of at most 0.011.
Values may be sent and summed in bfloat16 or wider, within the bound.
No kernel may reach another device: no remote copies, remote signals or barrier semaphores. Data moves between devices by JAX's collectives and lax.ppermute only.
A program may use at most 128 MiB of HBM per device.

```python
import math
import jax
import jax.numpy as jnp
import numpy as np
from jax import lax

D = 7168
FF = 1024
EXPERTS = 4
TOPF = 2
TOK_DEV = 64
CAP = 36
GROUP = 2
TOKENS = 512
N_SECTION = 4
N_EP = 8


def level_of(key, extent, pieces, smallest, largest):
    factor_of, own = 1.0, jax.random.fold_in(key, 6)
    for dim, blocks in pieces:
        heights = jnp.exp(jax.random.uniform(jax.random.fold_in(own, dim), (blocks,), jnp.float32, smallest / len(pieces), largest / len(pieces)))
        factor_of = factor_of * jnp.repeat(heights, extent[dim] // blocks).reshape([-1 if axis == dim else 1 for axis in range(len(extent))])
    return factor_of


def shared_out(own_key, own, number, rows, number_of, top, most, lean):
    ranking = jax.random.permutation(own_key, number_of)
    crowded, common = load_shares(number_of, rows * top, most, lean, True), load_shares(number_of, rows * top, most, lean, False)
    places = jnp.arange(number_of)

    def named(sizes, offset_by):
        used = int((sizes > 0).sum())
        fixed = max(1, used // 4)
        moved = fixed + (places - fixed + offset_by * (used - fixed)) % max(1, number_of - fixed)
        return jnp.zeros((number_of,), jnp.int32).at[ranking[jnp.where(places < fixed, places, moved)]].set(jnp.asarray(sizes, jnp.int32))

    sizes = jnp.where(number % 4 == 0, named(crowded, number // 4), named(common, number - number // 4 - 1))
    mixed = jax.random.permutation(jax.random.fold_in(own, 3), number_of)
    giver, sink = mixed[0:number_of // 2 * 2:2], mixed[1:number_of // 2 * 2:2]
    margin = jnp.minimum(sizes[giver] - 1, most - sizes[sink]) // 2
    margin = jnp.where((giver == ranking[0]) | (sink == ranking[0]) | (sizes[sink] == 0), 0, jnp.maximum(margin, 0))
    moved = jax.random.randint(jax.random.fold_in(own, 4), (number_of // 2,), 0, 1 << 20) % (margin + 1)
    sizes = sizes.at[giver].add(-moved).at[sink].add(moved)
    labels = jnp.searchsorted(jnp.cumsum(sizes), jnp.arange(rows * top), side="right").astype(jnp.int32)
    listing = labels.reshape(top, rows).T
    listing = listing[jax.random.permutation(jax.random.fold_in(own, 1), rows)]
    offset_by = jax.random.randint(jax.random.fold_in(own, 2), (rows, 1), 0, top)
    return jnp.take_along_axis(listing, (jnp.arange(top)[None, :] + offset_by) % top, axis=1)


def load_shares(amount, total, reach, lean, full):
    portions = [(1 << 20) // math.isqrt(rank ** lean) + 1 for rank in range(1, amount + 1)]
    largest = reach if full else min(reach, max(-(-total // amount), total * portions[0] // sum(portions)))
    least = 1 if total - largest >= amount - 1 else 0
    given, surplus = [largest] + [least] * (amount - 1), total - largest - least * (amount - 1)
    while surplus > 0:
        movable = [i for i in range(1, amount) if given[i] < largest] or [i for i in range(1, amount) if given[i] < reach]
        mass, remaining = sum([portions[i] for i in movable]), surplus
        for i in movable:
            more = min(reach - given[i], max(1, remaining * portions[i] // mass), surplus)
            given[i] = given[i] + more
            surplus = surplus - more
    return np.array(given)


def noise(stream_key, dims, deviation, most, pieces=(), kind=jnp.bfloat16):
    drawn = jax.random.normal(stream_key, dims, jnp.float32) * deviation
    if len(pieces) > 0:
        drawn = level_of(stream_key, dims, pieces, -0.22, 0.18) * drawn
    return jnp.clip(drawn, min=-most, max=most).astype(kind)


def setup_inputs(seed: int = 0) -> dict:
    key_list = jax.random.split(jax.random.key(seed), 10)
    handed = noise(key_list[0], (N_SECTION, 2, TOKENS, D), 1.0, 6.0, ((0, 4), (2, 8)))
    routes_keys = jax.random.split(jax.random.fold_in(key_list[1], 1), N_SECTION * 2 * TOKENS // TOK_DEV)
    routes_turns = jax.random.permutation(jax.random.fold_in(key_list[1], 3), N_SECTION * 2 * TOKENS // TOK_DEV)
    routes = jax.vmap(lambda own, number: shared_out(jax.random.fold_in(key_list[1], 2), own, number, TOK_DEV, EXPERTS, TOPF, CAP, 1))(routes_keys, routes_turns).reshape((N_SECTION, 2, TOKENS, TOPF))
    slot_order = jax.vmap(lambda own: jax.random.permutation(own, TOK_DEV))(jax.random.split(key_list[2], N_SECTION * 2 * N_EP)).reshape((N_SECTION, 2, N_EP, TOK_DEV)).astype(jnp.int32)
    gate_probs = jnp.clip(0.2 + 0.8 * jax.random.uniform(key_list[3], (N_SECTION, 2, TOKENS, TOPF), jnp.float32) ** level_of(key_list[3], (N_SECTION, 2, TOKENS, TOPF), ((0, 4), (2, 8)), -0.2, 0.2), 0.2, 1.0)
    saved_gate = noise(key_list[4], (N_SECTION, 2, N_EP, N_EP, CAP, FF // GROUP), 1.0, 6.0, ((0, 4), (2, 8)))
    saved_up = noise(key_list[5], (N_SECTION, 2, N_EP, N_EP, CAP, FF // GROUP), 1.0, 6.0, ((0, 4), (2, 8)))
    w_gate = noise(key_list[6], (N_SECTION, N_EP, D // GROUP, FF), D ** -0.5, 0.0625, ((0, 4), (1, 8)))
    w_up = noise(key_list[7], (N_SECTION, N_EP, D // GROUP, FF), D ** -0.5, 0.0625, ((0, 4), (1, 8)))
    w_down = noise(key_list[8], (N_SECTION, N_EP, FF, D // GROUP), FF ** -0.5, 0.1875, ((0, 4), (1, 8)))
    return {"handed": handed, "routes": routes, "slot_order": slot_order, "gate_probs": gate_probs, "saved_gate": saved_gate, "saved_up": saved_up, "w_gate": w_gate, "w_up": w_up, "w_down": w_down}


def slot_table(routing, sequence):
    expert_ids = jnp.arange(EXPERTS, dtype=jnp.int32)
    picked = (routing[:, :, None] == expert_ids[None, None, :]).astype(jnp.int32)
    named_count = jnp.sum(picked, axis=1)
    before = (sequence[None, :] < sequence[:, None]).astype(jnp.int32)
    counts = jnp.sum(before[:, :, None] * named_count[None, :, :], axis=1)
    return jnp.sum(counts[:, None, :] * picked, axis=2).astype(jnp.int32)


def reference(handed, routes, slot_order, gate_probs, saved_gate, saved_up, w_gate, w_up, w_down):
    group_size = N_EP // EXPERTS
    row_share = D // group_size
    unit_share = FF // group_size
    arriving = jnp.stack([jnp.roll(handed[:, 0], -1, axis=0), jnp.roll(handed[:, 1], 1, axis=0)], axis=1)
    sources = jnp.broadcast_to(jnp.arange(N_EP, dtype=jnp.int32)[:, None, None], (N_EP, TOK_DEV, TOPF))
    sections = []
    for section_index in range(N_SECTION):
        gate_full = w_gate[section_index].reshape(EXPERTS, D, FF).astype(jnp.float32)
        up_full = w_up[section_index].reshape(EXPERTS, D, FF).astype(jnp.float32)
        down_full = w_down[section_index].reshape(EXPERTS, group_size, FF, row_share)
        down_full = down_full.transpose(0, 2, 1, 3).reshape(EXPERTS, FF, D).astype(jnp.float32)
        directions = []
        for direction in range(2):
            grads = arriving[section_index, direction].reshape(N_EP, TOK_DEV, D)
            routing = routes[section_index, direction].reshape(N_EP, TOK_DEV, TOPF)
            slots = jax.vmap(slot_table)(routing, slot_order[section_index, direction])
            probs_here = gate_probs[section_index, direction].reshape(N_EP, TOK_DEV, TOPF)
            scaled = (probs_here[:, :, :, None] * grads[:, :, None, :].astype(jnp.float32)).astype(jnp.bfloat16)
            buffer = jnp.zeros((EXPERTS, N_EP, CAP, D), jnp.bfloat16).at[routing, sources, slots].set(scaled)
            row_block = buffer.reshape(EXPERTS, N_EP * CAP, D).astype(jnp.float32)
            hidden_grad = jnp.einsum("erd,efd->erf", row_block, down_full, precision=lax.Precision.HIGHEST)
            gate_vals = saved_gate[section_index, direction].reshape(EXPERTS, group_size, N_EP, CAP, unit_share)
            gate_vals = gate_vals.transpose(0, 2, 3, 1, 4).reshape(EXPERTS, N_EP * CAP, FF).astype(jnp.float32)
            up_vals = saved_up[section_index, direction].reshape(EXPERTS, group_size, N_EP, CAP, unit_share)
            up_vals = up_vals.transpose(0, 2, 3, 1, 4).reshape(EXPERTS, N_EP * CAP, FF).astype(jnp.float32)
            sigma = jax.nn.sigmoid(gate_vals)
            up_grad = (hidden_grad * gate_vals * sigma).astype(jnp.bfloat16)
            gate_grad = (hidden_grad * up_vals * sigma * (1.0 + gate_vals * (1.0 - sigma))).astype(jnp.bfloat16)
            combined = jnp.einsum("erf,edf->erd", gate_grad.astype(jnp.float32), gate_full, precision=lax.Precision.HIGHEST)
            combined = combined + jnp.einsum("erf,edf->erd", up_grad.astype(jnp.float32), up_full, precision=lax.Precision.HIGHEST)
            combined = combined.astype(jnp.bfloat16).reshape(EXPERTS, N_EP, CAP, D)
            picked_rows = combined[routing, sources, slots]
            summed = jnp.sum(picked_rows.astype(jnp.float32), axis=2).astype(jnp.bfloat16)
            directions.append(summed.reshape(N_EP * TOK_DEV, D))
        sections.append(jnp.stack(directions))
    return jnp.stack(sections)
```

```python
import jax
import jax.numpy as jnp
from jax import lax
from jax.sharding import PartitionSpec as P


EXPERTS = 4
CAP = 36
LANES = 128
SHARES = (0, 10, 28)
CHUNKS = len(SHARES) - 1


def partner(value, mask):
    pairs = [(source, source ^ mask) for source in range(lax.axis_size("ep"))]
    return lax.ppermute(value, "ep", pairs)


def relayed(value, steps, mask):
    sections, ranks = lax.axis_size("section"), lax.axis_size("ep")
    pairs = [
        (s * ranks + r, ((s + steps) % sections) * ranks + (r ^ mask))
        for s in range(sections)
        for r in range(ranks)
    ]
    return lax.ppermute(value, ("section", "ep"), pairs)


def slot_table(routing, sequence):
    expert_ids = jnp.arange(EXPERTS, dtype=jnp.int32)
    picked = (routing[:, :, None] == expert_ids[None, None, :]).astype(jnp.int32)
    named_count = jnp.sum(picked, axis=1)
    before = (sequence[None, :] < sequence[:, None]).astype(jnp.int32)
    counts = jnp.sum(before[:, :, None] * named_count[None, :, :], axis=1)
    return jnp.sum(counts[:, None, :] * picked, axis=2)


def halve_sums(partial_value, group, position):
    rows, width = partial_value.shape
    levels = group.bit_length() - 1
    current = partial_value.reshape((rows,) + (2,) * levels + (width // group,))
    for bit in range(levels - 1, -1, -1):
        axis = 1 + levels - 1 - bit
        half = position >> bit & 1
        kept = lax.dynamic_slice_in_dim(current, half, 1, axis=axis)
        given = lax.dynamic_slice_in_dim(current, 1 - half, 1, axis=axis)
        current = kept + partner(given, 1 << bit)
    return current.reshape(rows, width // group)


def gather_parts(pieces, group, position):
    levels = group.bit_length() - 1
    leading, width = pieces.shape[:-1], pieces.shape[-1]
    current = pieces.reshape(leading + (1,) * levels + (width,))
    for bit in range(levels):
        axis = len(leading) + levels - 1 - bit
        other = partner(current, 1 << bit)
        half = position >> bit & 1
        triple = jnp.concatenate([other, current, other], axis=axis)
        current = lax.dynamic_slice_in_dim(triple, 1 - half, 2, axis=axis)
    return current.reshape(leading + (width * group,))


def chunk_bounds(width):
    tiles = width // LANES
    edges = [tiles * part // SHARES[-1] * LANES for part in SHARES]
    return [(a, b - a) for a, b in zip(edges[:-1], edges[1:])]


def passes(handed, routes, slot_order, gate_probs, saved_gate, saved_up, w_gate, w_up, w_down):
    group = lax.axis_size("ep") // EXPERTS
    rank = lax.axis_index("ep")
    expert, member = rank // group, rank % group
    tokens, model_width = handed.shape[2], handed.shape[3]
    width = model_width // group
    bounds = chunk_bounds(width)
    rows = EXPERTS * group * CAP
    w_gate, w_up, w_down = w_gate[0, 0], w_up[0, 0], w_down[0, 0]

    slots = jax.vmap(slot_table)(routes[0], slot_order[0, :, 0])
    target = (routes[0] * CAP + slots).astype(jnp.float32)
    facts = jnp.stack([target, gate_probs[0]])
    facts = [facts] + [partner(facts, k) for k in range(1, group)]
    row_ids = jnp.arange(rows, dtype=jnp.int32)
    picks, scales, homes = [], [], []
    for d in range(2):
        hits, scale, home = [], 0.0, []
        for k in range(group):
            aim = facts[k][0, d].astype(jnp.int32)
            row = ((aim // CAP) ^ expert) * (group * CAP) + (member ^ k) * CAP + aim % CAP
            hit = row[None, :, :] == row_ids[:, None, None]
            scale = scale + jnp.sum(jnp.where(hit, facts[k][1, d][None], 0.0), axis=(1, 2))
            hits.append(jnp.any(hit, axis=2))
            home.append(row)
        picks.append(jnp.concatenate(hits, axis=1).astype(jnp.bfloat16))
        scales.append(scale[:, None])
        home = jnp.concatenate(home, axis=0)
        homes.append([])
        for c in range(CHUNKS):
            own_home, shift = lax.optimization_barrier((home + c * rows, jnp.int32(c * rows)))
            places = jnp.any(own_home[:, :, None] == row_ids[None, None, :] + shift, axis=1)
            homes[d].append(places.astype(jnp.bfloat16))

    def ordered(saved):
        blocks = saved.reshape(EXPERTS, group * CAP, saved.shape[-1])
        parts = [
            lax.dynamic_index_in_dim(blocks, expert ^ k, axis=0, keepdims=False)
            for k in range(EXPERTS)
        ]
        return jnp.concatenate(parts, axis=0).astype(jnp.float32)

    def across(value):
        blocks = value.reshape(EXPERTS, group * CAP, value.shape[-1])
        parts = [blocks[0]]
        for k in range(1, EXPERTS):
            parts.append(partner(blocks[k], k * group))
        return jnp.concatenate(parts, axis=0)

    def dispatched(d, steps, gates):
        sent = []
        for c, (start, size) in enumerate(bounds):
            pieces = []
            for k in range(group):
                piece = lax.dynamic_slice(
                    handed[0, d], (0, (member ^ k) * width + start), (tokens, size)
                )
                if gates:
                    piece, _ = lax.optimization_barrier((piece, gates[c]))
                pieces.append(relayed(piece, steps, k))
            gathered = jnp.concatenate(pieces, axis=0)
            picked = jnp.dot(picks[d], gathered, preferred_element_type=jnp.float32)
            sent.append((picked * scales[d]).astype(jnp.bfloat16))
        return sent, [across(rows_of) for rows_of in sent]

    def worked(d, arrived):
        partial_value = 0.0
        for c, (start, size) in enumerate(bounds):
            partial_value = partial_value + jnp.einsum(
                "rd,fd->rf",
                arrived[c],
                w_down[:, start : start + size],
                preferred_element_type=jnp.float32,
            )
        hidden_grad = halve_sums(partial_value, group, member)
        gate_float, up_float = ordered(saved_gate[0, d, 0]), ordered(saved_up[0, d, 0])
        sigma = jax.nn.sigmoid(gate_float)
        up_grad = hidden_grad * gate_float * sigma
        gate_grad = hidden_grad * up_float * sigma * (1.0 + gate_float * (1.0 - sigma))
        both = gather_parts(
            jnp.stack([gate_grad, up_grad]).astype(jnp.bfloat16), group, member
        )
        results = []
        for start, size in bounds:
            result = jnp.einsum(
                "rf,df->rd",
                both[0],
                w_gate[start : start + size],
                preferred_element_type=jnp.float32,
            )
            result = result + jnp.einsum(
                "rf,df->rd",
                both[1],
                w_up[start : start + size],
                preferred_element_type=jnp.float32,
            )
            results.append(result.astype(jnp.bfloat16))
        return results, [across(part) for part in results]

    def combined(d, returned):
        pieces = [[] for _ in range(group)]
        for c, (start, size) in enumerate(bounds):
            summed = jnp.einsum(
                "tr,rd->td", homes[d][c], returned[c], preferred_element_type=jnp.float32
            ).astype(jnp.bfloat16)
            summed = summed.reshape(group, tokens, size)
            pieces[0].append(summed[0])
            for k in range(1, group):
                pieces[k].append(partner(summed[k], k))
        stacked = jnp.stack([jnp.concatenate(p, axis=1) for p in pieces])
        out = [
            lax.dynamic_index_in_dim(stacked, member ^ a, axis=0, keepdims=False)
            for a in range(group)
        ]
        return jnp.concatenate(out, axis=1)

    sent_0, arrived_0 = dispatched(0, -1, None)
    _, arrived_1 = dispatched(1, 1, sent_0)
    _, returned_0 = worked(0, arrived_0)
    _, returned_1 = worked(1, arrived_1)
    outs = [combined(0, returned_0), combined(1, returned_1)]
    return jnp.stack(outs)[None]


def solution(mesh):
    in_specs = (
        P("section", None, "ep", None),
        P("section", None, "ep", None),
        P("section", None, "ep", None),
        P("section", None, "ep", None),
        P("section", None, "ep", None, None, None),
        P("section", None, "ep", None, None, None),
        P("section", "ep", None, None),
        P("section", "ep", None, None),
        P("section", "ep", None, None),
    )
    out_specs = P("section", None, "ep", None)
    return jax.shard_map(passes, mesh=mesh, in_specs=in_specs, out_specs=out_specs, check_vma=False)
```
